512 devices in a mesh: aisle: 32 (over z_hi, y), span: 16 (over x, z_lo, core).
Axes of the slice: x: 4, y: 8, z: 8 (z_hi: 4, z_lo: 2; z = z_hi * 2 + z_lo), core: 2. Of those that a mesh axis runs over, the one named last changes fastest.
Arguments:
- downflow_motion: float32 [512, 512, 256], P('aisle', 'span'), may hold values from -6 to 6
- crossflow_motion: float32 [512, 512, 256], P('aisle', 'span'), may hold values from -6 to 6
- upright_motion: float32 [512, 512, 256], P('aisle', 'span'), may hold values from -6 to 6
- thermal_anomaly: float32 [512, 512, 256], P('aisle', 'span'), may hold values from -6 to 6
- height_to_eigenbasis: float32 [256, 256], replicated, may hold values from -1 to 2
- eigenbasis_to_height: float32 [256, 256], replicated, may hold values from -1 to 2
- negated_height_spectrum: float32 [256], replicated, may hold values from 0.002 to 0.02
Outputs:
- east_after: float32 [512, 512, 256], P('aisle', 'span')
- north_after: float32 [512, 512, 256], P('aisle', 'span')
- upward_after: float32 [512, 512, 256], P('aisle', 'span')
- heat_after: float32 [512, 512, 256], P('aisle', 'span')
The draws below stay inside these ranges and needn't reach their ends.
All inputs are finite; a program needn't handle non-finite values.
Results may differ from the reference program's by a relative error of at most 0.0003.
Values sent between devices are 32-bit elements; how exact they have to be, the bound alone decides.
No kernel may reach another device: no remote copies, remote signals or barrier semaphores. Data moves between devices by JAX's collectives and lax.ppermute only.
A program may use at most 128 MiB of HBM per device.

```python
import math
import jax
import jax.numpy as jnp
from jax import lax

DOWNFLOW_POINTS = 512
CROSSFLOW_POINTS = 512
GAP_POINTS = 256


def wind_field(key, salt):
    inner = jax.random.fold_in(key, salt)
    shape = (DOWNFLOW_POINTS, CROSSFLOW_POINTS, GAP_POINTS)
    return jax.random.truncated_normal(inner, -6.0, 6.0, shape, jnp.float32)


def draw_downflow_motion(key, part):
    return wind_field(key, 31)


def draw_crossflow_motion(key, part):
    return wind_field(key, 37)


def draw_height_to_eigenbasis(key, part):
    inner = jax.random.fold_in(key, 11)
    noise = jax.random.truncated_normal(inner, -4.0, 4.0, (GAP_POINTS, GAP_POINTS), jnp.float32)
    return jnp.eye(GAP_POINTS, dtype=jnp.float32) + 0.35 / math.sqrt(GAP_POINTS) * noise


def draw_eigenbasis_to_height(key, part):
    inner = jax.random.fold_in(key, 23)
    noise = jax.random.truncated_normal(inner, -4.0, 4.0, (GAP_POINTS, GAP_POINTS), jnp.float32)
    return jnp.eye(GAP_POINTS, dtype=jnp.float32) + 0.35 / math.sqrt(GAP_POINTS) * noise


def levels(key, dims, cuts, least, top_value):
    loudness = 1.0
    for position, shards_of in cuts:
        draws = jax.random.uniform(jax.random.fold_in(jax.random.fold_in(key, 6), position), (shards_of,), jnp.float32, least / len(cuts), top_value / len(cuts))
        loudness = loudness * jnp.repeat(jnp.exp(draws), dims[position] // shards_of).reshape((-1,) + (1,) * (len(dims) - 1 - position))
    return loudness


def gaussian(key, shape, spread, limit, shards=(), kind=jnp.bfloat16):
    drawn = jax.random.normal(key, shape, jnp.float32) * spread
    if len(shards) > 0:
        drawn = levels(key, shape, shards, -0.22, 0.18) * drawn
    return jnp.clip(drawn, min=-limit, max=limit).astype(kind)


def setup_inputs(seed: int = 0) -> dict:
    key_list = jax.random.split(jax.random.key(seed), 8)
    return {
        "downflow_motion": draw_downflow_motion(jax.random.fold_in(key_list[7], 71), 0),
        "crossflow_motion": draw_crossflow_motion(jax.random.fold_in(key_list[7], 71), 0),
        "upright_motion": gaussian(key_list[2], (DOWNFLOW_POINTS, CROSSFLOW_POINTS, GAP_POINTS), 1.0, 6.0, ((0, 32), (1, 16)), jnp.float32),
        "thermal_anomaly": gaussian(key_list[3], (DOWNFLOW_POINTS, CROSSFLOW_POINTS, GAP_POINTS), 1.0, 6.0, ((0, 32), (1, 16)), jnp.float32),
        "height_to_eigenbasis": draw_height_to_eigenbasis(jax.random.fold_in(key_list[7], 71), 0),
        "eigenbasis_to_height": draw_eigenbasis_to_height(jax.random.fold_in(key_list[7], 71), 0),
        "negated_height_spectrum": jnp.clip(jnp.exp(jax.random.uniform(key_list[6], (GAP_POINTS,), jnp.float32, math.log(0.002), math.log(0.02))), 0.002, 0.02),
    }


step_gain = 0.1 * 8.0 / 15.0
viscosity = 0.01
smagorinsky = 0.05
prandtl = 0.7
buoyancy = 1.0
strain_floor = 0.25
highest = lax.Precision.HIGHEST

def predictor(padded):
    centre = padded[:, 1:-1, 1:-1, 1:-1]
    east_side = padded[:, 2:, 1:-1, 1:-1]
    west_side = padded[:, :-2, 1:-1, 1:-1]
    north_side = padded[:, 1:-1, 2:, 1:-1]
    south_side = padded[:, 1:-1, :-2, 1:-1]
    upper_side = padded[:, 1:-1, 1:-1, 2:]
    lower_side = padded[:, 1:-1, 1:-1, :-2]
    slope_east = 0.5 * (east_side - west_side)
    slope_north = 0.5 * (north_side - south_side)
    slope_upward = 0.5 * (upper_side - lower_side)
    laplace = east_side + west_side + (north_side + south_side) + (upper_side + lower_side) - 6.0 * centre
    strain = lax.optimization_barrier(jnp.sum(slope_east[:3] * slope_east[:3] + slope_north[:3] * slope_north[:3] + slope_upward[:3] * slope_upward[:3], axis=0))
    turbulent = viscosity + smagorinsky * jnp.sqrt(strain + strain_floor)
    transport = centre[0] * slope_east + centre[1] * slope_north + centre[2] * slope_upward
    diffusive = jnp.stack([turbulent, turbulent, turbulent, turbulent / prandtl])
    tendency = diffusive * laplace - transport
    tendency = jnp.concatenate([tendency[:2], tendency[2:3] + buoyancy * centre[3:4], tendency[3:]], axis=0)
    return centre + step_gain * tendency

def reference(downflow_motion, crossflow_motion, upright_motion, thermal_anomaly, height_to_eigenbasis, eigenbasis_to_height, negated_height_spectrum):
    bundled_unknowns = jnp.stack([downflow_motion, crossflow_motion, upright_motion, thermal_anomaly])
    padded = jnp.pad(bundled_unknowns, ((0, 0), (1, 1), (1, 1), (0, 0)), mode='wrap')
    padded = jnp.pad(padded, ((0, 0), (0, 0), (0, 0), (1, 1)))
    slab_size = math.gcd(DOWNFLOW_POINTS, 16)

    def one_slab(start):
        block = lax.dynamic_slice_in_dim(padded, start * slab_size, slab_size + 2, axis=1)
        return predictor(block)
    pieces = lax.map(one_slab, jnp.arange(DOWNFLOW_POINTS // slab_size, dtype=jnp.int32))
    predicted = jnp.moveaxis(pieces, 0, 1).reshape(4, DOWNFLOW_POINTS, CROSSFLOW_POINTS, GAP_POINTS)
    east_star = predicted[0]
    north_star = predicted[1]
    upward_star = predicted[2]
    heat_star = predicted[3]
    below = jnp.pad(upward_star[:, :, :-1], ((0, 0), (0, 0), (1, 0)))
    source = (east_star - jnp.roll(east_star, 1, axis=0) + (north_star - jnp.roll(north_star, 1, axis=1)) + (upward_star - below)) / step_gain
    vertical_modes = jnp.einsum('xyz,kz->xyk', source, height_to_eigenbasis, precision=highest)
    spectrum = jnp.fft.fft2(vertical_modes, axes=(0, 1))
    wave_x = jnp.sin(jnp.pi * jnp.arange(DOWNFLOW_POINTS, dtype=jnp.float32) / DOWNFLOW_POINTS)
    wave_y = jnp.sin(jnp.pi * jnp.arange(CROSSFLOW_POINTS, dtype=jnp.float32) / CROSSFLOW_POINTS)
    divisor = (-4.0 * wave_x * wave_x)[:, None, None] + (-4.0 * wave_y * wave_y)[None, :, None] - negated_height_spectrum[None, None, :]
    solved = jnp.real(jnp.fft.ifft2(spectrum / divisor, axes=(0, 1))).astype(downflow_motion.dtype)
    pressure = jnp.einsum('xyk,zk->xyz', solved, eigenbasis_to_height, precision=highest)
    above = jnp.pad(pressure[:, :, 1:], ((0, 0), (0, 0), (0, 1)))
    east_after = east_star - step_gain * (jnp.roll(pressure, -1, axis=0) - pressure)
    north_after = north_star - step_gain * (jnp.roll(pressure, -1, axis=1) - pressure)
    upward_after = upward_star - step_gain * (above - pressure)
    return (east_after, north_after, upward_after, heat_star)
```

```python
import math

import jax
import jax.numpy as jnp
import numpy as np
from jax import lax
from jax.experimental import pallas as pl
from jax.experimental.pallas import tpu as pltpu
from jax.sharding import PartitionSpec as P

step_gain = 0.1 * 8.0 / 15.0
viscosity = 0.01
smagorinsky = 0.05
prandtl = 0.7
buoyancy = 1.0
strain_floor = 0.25

f32 = jnp.float32
bf16 = jnp.bfloat16

NX, NY, NZ = 16, 32, 256
SHARE = 16
GROUPS = 16
RINGS = 32
LINE = NY * GROUPS
LANES = 128
PACK = 72


def fourier_table(length):
    wave = np.arange(length)[:, None]
    cells = np.arange(length)[None, :]
    half = length // 2
    freq = np.where(wave <= half, wave, wave - half)
    angle = 2.0 * np.pi / length * (freq * cells % length)
    return np.where(wave <= half, np.cos(angle), np.sin(angle))


def halves(value):
    high = value.astype(bf16)
    low = (value - high.astype(f32)).astype(bf16)
    return high, low


def product(left, right, dims):
    dot = lambda a, b: lax.dot_general(a, b, (dims, ((), ())), preferred_element_type=f32)
    return dot(left[0], right[0]) + (dot(left[0], right[1]) + dot(left[1], right[0]))


def lane_of(shape):
    return lax.broadcasted_iota(jnp.int32, shape, len(shape) - 1)


def blocks_swapped(pieces):
    shape = pieces[0].shape
    lane = lane_of(shape)
    low = lane < 64
    even = (lane // 32) % 2 == 0
    a0, a1, a2, a3 = pieces
    r = lambda v, s: pltpu.roll(v, s, 1)
    b0 = jnp.where(low, a0, r(a2, 64))
    b2 = jnp.where(low, r(a0, 64), a2)
    b1 = jnp.where(low, a1, r(a3, 64))
    b3 = jnp.where(low, r(a1, 64), a3)
    c0 = jnp.where(even, b0, r(b1, 32))
    c1 = jnp.where(even, r(b0, 96), b1)
    c2 = jnp.where(even, b2, r(b3, 32))
    c3 = jnp.where(even, r(b2, 96), b3)
    return [c0, c1, c2, c3]


def moved(value, shift):
    shift = shift % LANES
    return value if shift == 0 else pltpu.roll(value, shift, 1)


def outer_unpacked(tile):
    lane = lane_of(tile.shape)
    first = jnp.where(lane < 64, tile, 0.0)
    second = jnp.where(lane < 64, pltpu.roll(tile, 64, 1), 0.0)
    return jnp.concatenate([first, second], axis=0)


def outer_packed(value):
    return value[:8] + pltpu.roll(value[8:], 64, 1)


def predict_kernel(u_ref, v_ref, w_ref, t_ref, west_ref, east_ref, south_ref, north_ref, basis_ref,
                   es_ref, ns_ref, ws_ref, ts_ref, send_ref, source_ref):
    fields = (u_ref, v_ref, w_ref, t_ref)
    row = lax.broadcasted_iota(jnp.int32, (NY, NZ), 0)
    lane = lax.broadcasted_iota(jnp.int32, (NY, NZ), 1)
    source_ref[NX * NY:, :] = jnp.zeros((LANES, NZ), f32)

    def layer(x, west_of, east_of, previous):
        centre, slopes, laplaces = [], [], []
        for f in range(4):
            c = fields[f][x]
            we, ea = west_of(f), east_of(f)
            no = jnp.where(row == NY - 1, north_ref[f, x], pltpu.roll(c, NY - 1, 0))
            so = jnp.where(row == 0, south_ref[f, x], pltpu.roll(c, 1, 0))
            up = jnp.where(lane == NZ - 1, 0.0, pltpu.roll(c, NZ - 1, 1))
            lo = jnp.where(lane == 0, 0.0, pltpu.roll(c, 1, 1))
            centre.append(c)
            slopes.append((0.5 * (ea - we), 0.5 * (no - so), 0.5 * (up - lo)))
            laplaces.append(ea + we + (no + so) + (up + lo) - 6.0 * c)
        strain = None
        for f in range(3):
            sx, sy, sz = slopes[f]
            term = sx * sx + sy * sy + sz * sz
            strain = term if strain is None else strain + term
        turbulent = viscosity + smagorinsky * jnp.sqrt(strain + strain_floor)
        stars = []
        for f in range(4):
            sx, sy, sz = slopes[f]
            k = turbulent if f < 3 else turbulent * (1.0 / prandtl)
            tendency = k * laplaces[f] - (centre[0] * sx + centre[1] * sy + centre[2] * sz)
            if f == 2:
                tendency = tendency + buoyancy * centre[3]
            stars.append(centre[f] + step_gain * tendency)
        es, ns, ws, ts = stars
        es_ref[x] = es
        ns_ref[x] = ns
        ws_ref[x] = ws
        ts_ref[x] = ts
        behind = jnp.where(row == 0, 0.0, pltpu.roll(ns, 1, 0))
        below = jnp.where(lane == 0, 0.0, pltpu.roll(ws, 1, 1))
        first = es if previous is None else es - previous
        source = (first + (ns - behind) + (ws - below)) * (1.0 / step_gain)
        start = x * NY if isinstance(x, int) else pl.multiple_of(x * NY, NY)
        source_ref[pl.ds(start, NY), :] = source
        source_ref[pl.ds(NX * NY + x, 1), :] = ns[NY - 1:NY, :] * (-1.0 / step_gain)
        return es

    layer(0, lambda f: west_ref[f], lambda f: fields[f][1], None)

    def middle(x, carry):
        layer(x, lambda f: fields[f][x - 1], lambda f: fields[f][x + 1], es_ref[x - 1])
        return carry

    lax.fori_loop(1, NX - 1, middle, 0)
    last = layer(NX - 1, lambda f: fields[f][NX - 2], lambda f: east_ref[f], es_ref[NX - 2])
    source_ref[NX * NY + 32:NX * NY + 64, :] = last * (-1.0 / step_gain)

    modes = product(halves(basis_ref[...]), halves(source_ref[...]), ((1,), (1,)))
    for g in range(GROUPS):
        rows = slice(g * SHARE, (g + 1) * SHARE)
        for block in range(4):
            send_ref[g, block * 16:(block + 1) * 16, :] = modes[rows, block * LANES:(block + 1) * LANES]
        send_ref[g, 64:PACK, :] = outer_packed(modes[rows, 4 * LANES:])


def lines_kernel(recv_ref, table_high_ref, table_low_ref, ratio_ref, lines_ref, moments_ref, work_ref):
    shape = (SHARE, LANES)
    lane = lane_of(shape)
    outer = [outer_unpacked(recv_ref[b, 64:PACK, :]) for b in range(GROUPS)]
    for bg in range(4):
        column = slice(bg * LANES, (bg + 1) * LANES)
        along_y = jnp.zeros(shape, f32)
        along_x = jnp.zeros(shape, f32)
        for bi in range(4):
            b = bg * 4 + bi
            inside = (lane // 32) == bi
            along_y = jnp.where(inside, moved(outer[(b - 1) % GROUPS], bi * 32), along_y)
            along_x = jnp.where(inside, moved(outer[b], bi * 32 - 32), along_x)
        work_ref[NX * SHARE:, column] = along_x
        for block in range(4):
            pieces = [recv_ref[bg * 4 + bi, block * 16:(block + 1) * 16, :] for bi in range(4)]
            for xi, piece in enumerate(blocks_swapped(pieces)):
                x = block * 4 + xi
                piece = piece + jnp.where(lane % 32 == 0, moved(along_y, -x), 0.0)
                work_ref[x * SHARE:(x + 1) * SHARE, column] = piece
    table = (table_high_ref[...], table_low_ref[...])
    lines_ref[...] = product(halves(work_ref[...]), table, ((1,), (1,)))
    for block in range(4):
        column = slice(block * LANES, (block + 1) * LANES)
        cells = [lines_ref[x * SHARE:(x + 1) * SHARE, column] for x in range(NX + 1)]
        ratio = ratio_ref[:, column]
        ahead = cells[0]
        for x in range(1, NX + 1):
            ahead = cells[x] + ratio * ahead
        back = cells[NX]
        for x in range(NX - 1, -1, -1):
            back = cells[x] + ratio * back
        moments_ref[block * 16:(block + 1) * 16, :] = ahead
        moments_ref[64 + block * 16:64 + (block + 1) * 16, :] = back


def chain_kernel(moments_ref, power_ref, closing_ref, forward_ref, out_ref):
    power = power_ref[...]
    closing = closing_ref[...]
    forward = forward_ref[...] > 0.5
    terms = [jnp.where(forward, moments_ref[m], moments_ref[RINGS - 1 - m]) for m in range(RINGS)]
    total = terms[0]
    for m in range(1, RINGS):
        total = terms[m] + power * total
    value = total * closing
    values = [value]
    for m in range(RINGS - 1):
        value = terms[m] + power * value
        values.append(value)
    for m in range(RINGS):
        out_ref[m] = jnp.where(forward, values[m], values[RINGS - 1 - m])


def solve_kernel(lines_ref, carry_ref, table_high_ref, table_low_ref, ratio_ref, gain_ref, send_ref, work_ref):
    shape = (SHARE, LANES)
    lane = lane_of(shape)
    for block in range(4):
        column = slice(block * LANES, (block + 1) * LANES)
        ratio = ratio_ref[:, column]
        gain = gain_ref[:, column]
        cells = [lines_ref[x * SHARE:(x + 1) * SHARE, column] for x in range(NX + 1)]
        back = [None] * (NX + 1)
        back[NX] = carry_ref[64 + block * 16:64 + (block + 1) * 16, :] + cells[NX]
        for x in range(NX - 1, 0, -1):
            back[x] = cells[x] + ratio * back[x + 1]
        ahead = carry_ref[block * 16:(block + 1) * 16, :] + cells[0]
        for x in range(NX):
            work_ref[x * SHARE:(x + 1) * SHARE, column] = gain * (ahead + ratio * back[x + 1])
            if x < NX - 1:
                ahead = cells[x + 1] + ratio * ahead
        work_ref[NX * SHARE:, column] = gain * (ratio * ahead + back[NX])
    table = (table_high_ref[...], table_low_ref[...])
    work_ref[...] = product(halves(work_ref[...]), table, ((1,), (0,)))
    along_y = []
    for bg in range(4):
        column = slice(bg * LANES, (bg + 1) * LANES)
        gathered = jnp.zeros(shape, f32)
        for x in range(NX):
            piece = work_ref[x * SHARE:(x + 1) * SHARE, column]
            gathered = jnp.where(lane % 32 == x, moved(piece, x), gathered)
        along_y.append(gathered)
        for block in range(4):
            pieces = [work_ref[x * SHARE:(x + 1) * SHARE, column] for x in range(block * 4, block * 4 + 4)]
            for bi, piece in enumerate(blocks_swapped(pieces)):
                send_ref[bg * 4 + bi, block * 16:(block + 1) * 16, :] = piece
    for b in range(GROUPS):
        bg, bi = b // 4, b % 4
        ng, ni = ((b + 1) % GROUPS) // 4, (b + 1) % 4
        along_x = work_ref[NX * SHARE:, bg * LANES:(bg + 1) * LANES]
        outer = jnp.where(lane < 16, moved(along_y[ng], -32 * ni), 0.0)
        outer = jnp.where((lane >= 32) & (lane < 64), moved(along_x, 32 - 32 * bi), outer)
        send_ref[b, 64:PACK, :] = outer_packed(outer)


def correct_kernel(recv_ref, basis_ref, es_ref, ns_ref, ws_ref, ea_ref, na_ref, wa_ref, modes_ref, pressure_ref):
    for b in range(GROUPS):
        rows = slice(b * SHARE, (b + 1) * SHARE)
        for block in range(4):
            modes_ref[rows, block * LANES:(block + 1) * LANES] = recv_ref[b, block * 16:(block + 1) * 16, :]
        modes_ref[rows, 4 * LANES:] = outer_unpacked(recv_ref[b, 64:PACK, :])
    pressure_ref[...] = product(halves(modes_ref[...].T), halves(basis_ref[...]), ((1,), (1,)))
    row = lax.broadcasted_iota(jnp.int32, (NY, NZ), 0)
    lane = lax.broadcasted_iota(jnp.int32, (NY, NZ), 1)

    def layer(x, carry):
        start = pl.multiple_of(x * NY, NY)
        here = pressure_ref[pl.ds(start, NY), :]
        after = pl.multiple_of(jnp.where(x == NX - 1, NX * NY + 32, start + NY), NY)
        ahead = pressure_ref[pl.ds(after, NY), :]
        beyond = pressure_ref[pl.ds(NX * NY + x, 1), :]
        north = jnp.where(row == NY - 1, beyond, pltpu.roll(here, NY - 1, 0))
        above = jnp.where(lane == NZ - 1, 0.0, pltpu.roll(here, NZ - 1, 1))
        ea_ref[x] = es_ref[x] - step_gain * (ahead - here)
        na_ref[x] = ns_ref[x] - step_gain * (north - here)
        wa_ref[x] = ws_ref[x] - step_gain * (above - here)
        return carry

    lax.fori_loop(0, NX, layer, 0)


def shifted(value, axis, steps):
    count = lax.axis_size(axis)
    return lax.ppermute(value, axis, [(i, (i + steps) % count) for i in range(count)])


def decay(shift):
    root = jnp.sqrt(shift + 0.25 * shift * shift)
    ratio = 1.0 / (1.0 + 0.5 * shift + root)
    return ratio, jnp.log1p(0.5 * shift + root), 2.0 * root


def call(kernel, outs, scratch=(), name=None):
    vmem = pl.BlockSpec(memory_space=pltpu.VMEM)
    return pl.pallas_call(
        kernel,
        out_shape=outs,
        out_specs=jax.tree.map(lambda _: vmem, outs),
        scratch_shapes=[pltpu.VMEM(shape, f32) for shape in scratch],
        compiler_params=pltpu.CompilerParams(vmem_limit_bytes=50 * 2**20),
        name=name,
    )


def shape_of(*dims):
    return jax.ShapeDtypeStruct(dims, f32)


def per_device(downflow_motion, crossflow_motion, upright_motion, thermal_anomaly,
               height_to_eigenbasis, eigenbasis_to_height, negated_height_spectrum):
    fields = (downflow_motion, crossflow_motion, upright_motion, thermal_anomaly)
    west = shifted(jnp.stack([f[NX - 1] for f in fields]), "aisle", 1)
    east = shifted(jnp.stack([f[0] for f in fields]), "aisle", -1)
    south = shifted(jnp.stack([f[:, NY - 1:] for f in fields]), "span", 1)
    north = shifted(jnp.stack([f[:, :1] for f in fields]), "span", -1)

    exact = fourier_table(LINE)
    table_high = np.asarray(exact, np.float32).astype(bf16)
    table_low = (exact - table_high.astype(np.float64)).astype(np.float32).astype(bf16)
    table_high, table_low = jnp.asarray(table_high), jnp.asarray(table_low)

    wave = np.arange(LINE)
    freq = np.where(wave <= LINE // 2, wave, wave - LINE // 2)
    eigen = jnp.asarray((4.0 * np.sin(np.pi / LINE * freq) ** 2).astype(np.float32))
    weight = jnp.asarray(np.where((wave == 0) | (wave == LINE // 2), 1.0 / LINE, 2.0 / LINE).astype(np.float32))
    here_x, here_y = lax.axis_index("aisle"), lax.axis_index("span")
    levels = lax.dynamic_slice_in_dim(negated_height_spectrum, here_y * SHARE, SHARE)
    ratio, _, gap = decay(eigen[None, :] + levels[:, None])
    gain = -weight[None, :] / gap
    part = here_x % 16
    some_levels = lax.dynamic_slice_in_dim(levels, (part % 4) * 4, 4)
    some_eigen = lax.dynamic_slice_in_dim(eigen, (part // 4) * LANES, LANES)
    _, exponent, _ = decay(some_eigen[None, :] + some_levels[:, None])
    power = jnp.exp(-NX * exponent)
    closing = -1.0 / jnp.expm1(-(NX * RINGS) * exponent)
    forward = jnp.broadcast_to((here_x < 16).astype(f32), (4, LANES))

    block = shape_of(NX, NY, NZ)
    es, ns, ws, ts, sent = call(
        predict_kernel, (block, block, block, block, shape_of(GROUPS, PACK, LANES)),
        [(NX * NY + LANES, NZ)], "predict",
    )(*fields, west, east, south, north, height_to_eigenbasis)
    held = lax.all_to_all(sent, "span", split_axis=0, concat_axis=0, tiled=True)
    lines, moments = call(
        lines_kernel, (shape_of((NX + 1) * SHARE, LINE), shape_of(RINGS * 4, LANES)),
        [((NX + 1) * SHARE, LINE)], "lines",
    )(held, table_high, table_low, ratio)
    moments = lax.all_to_all(moments.reshape(RINGS, 4, LANES), "aisle", split_axis=0, concat_axis=0, tiled=True)
    carry = call(chain_kernel, shape_of(RINGS, 4, LANES), (), "chain")(moments, power, closing, forward)
    carry = lax.all_to_all(carry, "aisle", split_axis=0, concat_axis=0, tiled=True)
    sent = call(
        solve_kernel, shape_of(GROUPS, PACK, LANES), [((NX + 1) * SHARE, LINE)], "solve",
    )(lines, carry.reshape(RINGS * 4, LANES), table_high, table_low, ratio, gain)
    held = lax.all_to_all(sent, "span", split_axis=0, concat_axis=0, tiled=True)
    ea, na, wa = call(
        correct_kernel, (block, block, block), [(NZ, 5 * LANES), (5 * LANES, NZ)], "correct",
    )(held, eigenbasis_to_height, es, ns, ws)
    return ea, na, wa, ts


def solution(mesh):
    cells = P("aisle", "span", None)
    return jax.shard_map(
        per_device,
        mesh=mesh,
        in_specs=(cells, cells, cells, cells, P(), P(), P()),
        out_specs=(cells, cells, cells, cells),
        check_vma=False,
    )
```
